32 devices in a mesh: groups: 2 (over x), seq: 16 (over z, y, core).
Axes of the slice: x: 2, y: 2, z: 4, core: 2. Of those that a mesh axis runs over, the one named last changes fastest.
Arguments:
- hidden: bfloat16 [16384, 320], P(('groups', 'seq')), parts along dimension 0, may hold values from -20 to 20
- ref_hidden: bfloat16 [2048, 320], P(('groups', 'seq')), parts along dimension 0, may hold values from -6 to 6
- visible: int32 [128, 64], P('groups'), parts along dimension 0, may hold values 0 or 1
- ref_count: int32 [2], P('groups'), parts along dimension 0, may hold values from 256 to 1024
- w_query: bfloat16 [320, 320], replicated, may hold values from -0.3125 to 0.3125
- w_key: bfloat16 [320, 320], replicated, may hold values from -0.3125 to 0.3125
- w_value: bfloat16 [320, 320], replicated, may hold values from -0.3125 to 0.3125
- w_out: bfloat16 [320, 320], replicated, may hold values from -0.3125 to 0.3125
Outputs:
- attended: bfloat16 [16384, 320], P(('groups', 'seq')), parts along dimension 0
The draws below stay inside these ranges and needn't reach their ends.
There are 2 independent parts, one for each index of `groups`. The reference program is written for one: setup_inputs(seed, part) draws one part's arguments, and reference() takes and returns one part's arrays. A program takes and returns all parts, laid end to end along the dimension named above; an argument that names none is the same for every part. Nothing has to cross between parts.
All inputs are finite; a program needn't handle non-finite values.
Results may differ from the reference program's by a relative error of at most 0.011.
Values may be sent and summed in bfloat16 or wider, within the bound.
A program may use at most 128 MiB of HBM per device.

```python
import jax
import jax.numpy as jnp
from jax import lax

HEADS = 5
HEAD_DIM = 64
D = 320
TILE = 128
TILES_VIEW = 8
TOKENS = 8192
REF_TOK = 1024
NT = 64


def draw_hidden(key, part):
    base_key = jax.random.fold_in(key, 11)
    values = jax.random.truncated_normal(base_key, -6.0, 6.0, (TOKENS, D), jnp.float32)
    return values.astype(jnp.bfloat16)


def touch_ends(result, key, low, high):
    place = [jax.random.randint(jax.random.fold_in(key, axis), (), 0, length) for axis, length in enumerate(result.shape)]
    main_axis = result.shape.index(max(result.shape))
    next_to = place[:main_axis] + [(place[main_axis] + 1) % result.shape[main_axis]] + place[main_axis + 1:]
    return result.at[tuple(place)].set(low).at[tuple(next_to)].set(high)


def levels(key, extent, cuts, least, top_value):
    factor_of, own = 1.0, jax.random.fold_in(key, 6)
    for axis_at, parts in cuts:
        steps = jnp.exp(jax.random.uniform(jax.random.fold_in(own, axis_at), (parts,), jnp.float32, least / len(cuts), top_value / len(cuts)))
        factor_of = factor_of * jnp.repeat(steps, extent[axis_at] // parts).reshape([-1 if axis == axis_at else 1 for axis in range(len(extent))])
    return factor_of


def centred(own_key, shape, width, reach, cuts=(), kind=jnp.bfloat16):
    level = levels(own_key, shape, cuts, -0.22, 0.18) if cuts else 1.0
    entries = jax.random.normal(own_key, shape, jnp.float32) * width * level
    return jnp.minimum(jnp.maximum(entries, -reach), reach).astype(kind)


def setup_inputs(seed: int = 0, part: int = 0) -> dict:
    key_list = jax.random.split(jax.random.key(seed), 9)
    part_splits = jax.random.split(jax.random.fold_in(key_list[8], part), 9)
    hidden = draw_hidden(jax.random.fold_in(jax.random.fold_in(key_list[8], part), 71), part)
    ref_hidden = centred(part_splits[1], (REF_TOK, D), 1.0, 6.0, ((0, 16),))
    visible = touch_ends((jax.random.randint(part_splits[2], (NT, NT), 0, 2) < 1).astype(jnp.int32), jax.random.fold_in(part_splits[2], 1), 0, 1)
    ref_count = jax.random.randint(part_splits[3], (1,), REF_TOK // 4, REF_TOK + 1).astype(jnp.int32)
    w_query = centred(key_list[4], (D, D), D ** -0.5, 0.3125)
    w_key = centred(key_list[5], (D, D), D ** -0.5, 0.3125)
    w_value = centred(key_list[6], (D, D), D ** -0.5, 0.3125)
    w_out = centred(key_list[7], (D, D), D ** -0.5, 0.3125)
    return dict(hidden=hidden, ref_hidden=ref_hidden, visible=visible, ref_count=ref_count, w_query=w_query, w_key=w_key, w_value=w_value, w_out=w_out)


def reference(hidden, ref_hidden, visible, ref_count, w_query, w_key, w_value, w_out):
    queries = jnp.dot(hidden, w_query, preferred_element_type=jnp.float32).astype(jnp.bfloat16)
    view_keys = jnp.dot(hidden, w_key, preferred_element_type=jnp.float32).astype(jnp.bfloat16)
    view_values = jnp.dot(hidden, w_value, preferred_element_type=jnp.float32).astype(jnp.bfloat16)
    ref_keys = jnp.dot(ref_hidden, w_key, preferred_element_type=jnp.float32).astype(jnp.bfloat16)
    ref_values = jnp.dot(ref_hidden, w_value, preferred_element_type=jnp.float32).astype(jnp.bfloat16)
    all_keys = jnp.concatenate([view_keys, ref_keys], 0).astype(jnp.float32).reshape(TOKENS + REF_TOK, HEADS, HEAD_DIM)
    all_values = jnp.concatenate([view_values, ref_values], 0).astype(jnp.float32).reshape(TOKENS + REF_TOK, HEADS, HEAD_DIM)
    key_tile = jnp.arange(TOKENS, dtype=jnp.int32) // TILE
    key_view = key_tile // TILES_VIEW
    ref_ok = jnp.arange(REF_TOK, dtype=jnp.int32) < ref_count[0]
    scale = 1.0 / (HEAD_DIM ** 0.5)

    def one_tile(tile_index):
        block = lax.dynamic_slice_in_dim(queries, tile_index * TILE, TILE, 0)
        block = block.astype(jnp.float32).reshape(TILE, HEADS, HEAD_DIM)
        row_visible = visible[tile_index]
        view_ok = (row_visible[key_tile] == 1) | (key_view == tile_index // TILES_VIEW)
        allowed = jnp.concatenate([view_ok, ref_ok], 0)
        scores = jnp.einsum("qhd,khd->hqk", block, all_keys) * scale
        scores = jnp.where(allowed[None, None, :], scores, jnp.float32(-1e30))
        row_max = jnp.max(scores, axis=-1, keepdims=True)
        expo = jnp.exp(scores - row_max)
        total = jnp.sum(expo, axis=-1)
        weights = expo.astype(jnp.bfloat16).astype(jnp.float32)
        mixed = jnp.einsum("hqk,khd->hqd", weights, all_values) / total[:, :, None]
        return jnp.transpose(mixed, (1, 0, 2)).reshape(TILE, HEADS * HEAD_DIM).astype(jnp.bfloat16)

    tiles_out = lax.map(one_tile, jnp.arange(NT, dtype=jnp.int32))
    mixed_all = tiles_out.reshape(TOKENS, HEADS * HEAD_DIM)
    return jnp.dot(mixed_all, w_out, preferred_element_type=jnp.float32).astype(jnp.bfloat16)
```

```python
import functools
import math

import jax
import jax.numpy as jnp
from jax import lax
from jax.experimental import pallas as pl
from jax.experimental.pallas import tpu as pltpu
from jax.sharding import PartitionSpec as P

HEADS = 5
TILE = 128
TILES_VIEW = 8
NEG = -1e30
F32 = jnp.float32
BF16 = jnp.bfloat16


def lanes(width):
    return -(-width // 128) * 128


def nt(a, b):
    return lax.dot_general(a, b, (((1,), (1,)), ((), ())), preferred_element_type=F32)


def tn(a, b):
    return lax.dot_general(a, b, (((0,), (0,)), ((), ())), preferred_element_type=F32)


def prepare(hidden_ref, visible_ref, wq_ref, wk_ref, wv_ref, wkp, wvt, qz, vis, m_s, acc_s, me):
    rows, width = hidden_ref.shape
    size = width // HEADS
    pad = lanes(width)
    shift = pad - width
    tiles = visible_ref.shape[0]
    wkp[...] = jnp.zeros_like(wkp)
    wkp[0, :width, :width] = wk_ref[...]
    wkp[1, shift:, :width] = wk_ref[...]
    wvt_val = wv_ref[...].T
    wvt[...] = jnp.zeros_like(wvt)
    wvt[0, :, :width] = wvt_val
    wvt[1, :, shift:] = wvt_val
    scale = math.log2(math.e) / math.sqrt(size)
    q = jnp.dot(hidden_ref[...], wq_ref[...], preferred_element_type=F32) * scale
    qt = q.T.astype(BF16)
    qz[...] = jnp.zeros_like(qz)
    for h in range(HEADS):
        base = (h % 2) * size
        qz[h, base:base + size, :] = qt[h * size:(h + 1) * size]
    first = me * (rows // TILE)
    q_tile = first + lax.broadcasted_iota(jnp.int32, (tiles, rows), 1) // TILE
    k_tile = lax.broadcasted_iota(jnp.int32, (tiles, rows), 0)
    pick = (k_tile == q_tile).astype(BF16)
    seen = tn(visible_ref[...].astype(F32).astype(BF16), pick)
    own = (q_tile // TILES_VIEW) == (k_tile // TILES_VIEW)
    vis[...] = jnp.where((seen > 0.5) | own, F32(1.0), F32(0.0))
    m_s[...] = jnp.full_like(m_s, NEG)
    acc_s[...] = jnp.zeros_like(acc_s)


def absorb(x, wkp, wvt, qz, m_s, acc_s, width, vis_rows, limit):
    size = width // HEADS
    pad = lanes(width)
    half = x.shape[0]
    x_lo, x_hi = x[:, :pad], x[:, 2 * width - pad:]
    keys = jnp.concatenate(
        [
            jnp.dot(x_lo, wkp[0], preferred_element_type=F32).astype(BF16),
            jnp.dot(x_hi, wkp[1], preferred_element_type=F32).astype(BF16),
        ],
        axis=0,
    )
    values = [nt(wvt[0], x_lo).astype(BF16), nt(wvt[1], x_hi).astype(BF16)]
    ones = jnp.ones((16, half), BF16)
    for h in range(HEADS):
        s = jnp.dot(
            keys[:, (h // 2) * 128:(h // 2) * 128 + 128], qz[h], preferred_element_type=F32
        )
        m_old = m_s[h:h + 1, :]
        if vis_rows is None:
            part, at_lo, at_hi = limit
            ids = lax.broadcasted_iota(jnp.int32, (half, 1), 0)
            s = jnp.where(jnp.concatenate([at_lo(ids), at_hi(ids)], axis=0) < part, s, NEG)
            m_new = jnp.maximum(m_old, jnp.max(s, axis=0, keepdims=True))
            p = jnp.exp2(s - m_new).astype(BF16)
        else:
            tops = []
            for t, ok in enumerate(vis_rows):
                top = jnp.max(s[t * TILE:(t + 1) * TILE], axis=0, keepdims=True)
                tops.append(jnp.where(ok, top, NEG))
            m_new = functools.reduce(jnp.maximum, tops, m_old)
            parts = []
            for t, ok in enumerate(vis_rows):
                less = jnp.where(ok, m_new, F32(-NEG))
                parts.append(jnp.exp2(s[t * TILE:(t + 1) * TILE] - less).astype(BF16))
            p = jnp.concatenate(parts, axis=0)
        fade = jnp.exp2(m_old - m_new)
        m_s[h:h + 1, :] = m_new
        total = acc_s[h] * fade
        for k in range(2):
            v = jnp.concatenate([values[k][h * size:(h + 1) * size], ones], axis=0)
            total = total + jnp.dot(
                v, p[k * half:(k + 1) * half], preferred_element_type=F32
            )
        acc_s[h] = total


def finish(out_ref, wo_ref, acc_s, width):
    size = width // HEADS
    out = None
    for h in range(HEADS):
        mixed = (acc_s[h, :size] / acc_s[h, size:size + 1]).T.astype(BF16)
        term = jnp.dot(mixed, wo_ref[h * size:(h + 1) * size], preferred_element_type=F32)
        out = term if out is None else out + term
    out_ref[...] = out.astype(BF16)


def kernel(count_ref, gathered_ref, hidden_ref, visible_ref, wq_ref, wk_ref, wv_ref, wo_ref,
           out_ref, wkp, wvt, qz, vis, m_s, acc_s, refs):
    n = gathered_ref.shape[0]
    rows, width = hidden_ref.shape
    half = rows // 2
    ref_half = gathered_ref.shape[1] - half
    me = lax.axis_index("seq")
    prepare(hidden_ref, visible_ref, wq_ref, wk_ref, wv_ref, wkp, wvt, qz, vis, m_s, acc_s, me)
    tiles = rows // TILE

    def step(i, carry):
        j = lax.rem(me + i, n)
        vis_rows = [vis[pl.ds(j * tiles + t, 1), :] > 0.5 for t in range(tiles)]
        absorb(gathered_ref[j, :half], wkp, wvt, qz, m_s, acc_s, width, vis_rows, None)
        return carry

    lax.fori_loop(0, n, step, 0)
    for j in range(n):
        refs[j * ref_half:(j + 1) * ref_half] = gathered_ref[j, half:]
    count = count_ref[0]
    block = half
    for b in range(n * ref_half // block):
        def at(ids, extra, b=b):
            r = ids + b * block
            return (r // ref_half) * (2 * ref_half) + r % ref_half + extra
        absorb(refs[b * block:(b + 1) * block], wkp, wvt, qz, m_s, acc_s, width, None,
               (count, lambda ids: at(ids, 0), lambda ids: at(ids, ref_half)))
    finish(out_ref, wo_ref, acc_s, width)


def pack(x):
    half = x.shape[0] // 2
    return jnp.concatenate([x[:half], x[half:]], axis=1)


def local(hidden, ref_hidden, visible, ref_count, w_query, w_key, w_value, w_out):
    rows, width = hidden.shape
    size = width // HEADS
    pad = lanes(width)
    mine = jnp.concatenate([pack(hidden), pack(ref_hidden)], axis=0)
    gathered = lax.all_gather(mine, "seq", axis=0, tiled=False)
    n = gathered.shape[0]
    vmem = pl.BlockSpec(memory_space=pltpu.VMEM)
    return pl.pallas_call(
        kernel,
        out_shape=jax.ShapeDtypeStruct((rows, width), BF16),
        in_specs=[pl.BlockSpec(memory_space=pltpu.SMEM)] + [vmem] * 7,
        out_specs=vmem,
        scratch_shapes=[
            pltpu.VMEM((2, pad, pad), BF16),
            pltpu.VMEM((2, width, pad), BF16),
            pltpu.VMEM((HEADS, 128, rows), BF16),
            pltpu.VMEM((visible.shape[0], rows), F32),
            pltpu.VMEM((8, rows), F32),
            pltpu.VMEM((HEADS, size + 16, rows), F32),
            pltpu.VMEM((n * ref_hidden.shape[0] // 2, 2 * width), BF16),
        ],
        compiler_params=pltpu.CompilerParams(vmem_limit_bytes=56 << 20),
    )(ref_count, gathered, hidden, visible, w_query, w_key, w_value, w_out)


def solution(mesh):
    in_specs = (
        P(("groups", "seq"), None),
        P(("groups", "seq"), None),
        P("groups", None),
        P("groups"),
        P(),
        P(),
        P(),
        P(),
    )
    out_specs = P(("groups", "seq"), None)
    return jax.shard_map(local, mesh=mesh, in_specs=in_specs, out_specs=out_specs, check_vma=False)
```

```python
import functools
import math

import jax
import jax.numpy as jnp
from jax import lax
from jax.experimental import pallas as pl
from jax.experimental.pallas import tpu as pltpu
from jax.sharding import PartitionSpec as P

HEADS = 5
TILE = 128
TILES_VIEW = 8
NEG = -1e30
F32 = jnp.float32
BF16 = jnp.bfloat16


def lanes(width):
    return -(-width // 128) * 128


def nt(a, b):
    return lax.dot_general(a, b, (((1,), (1,)), ((), ())), preferred_element_type=F32)


def tn(a, b):
    return lax.dot_general(a, b, (((0,), (0,)), ((), ())), preferred_element_type=F32)


def prepare(mine_ref, visible_ref, wq_ref, wk_ref, wv_ref, wkp, wvt, qz, vis, m_s, acc_s, me):
    rows = qz.shape[2]
    half = rows // 2
    width = mine_ref.shape[1] // 2
    size = width // HEADS
    pad = lanes(width)
    shift = pad - width
    tiles = visible_ref.shape[0]
    wkp[...] = jnp.zeros_like(wkp)
    wkp[0, :width, :width] = wk_ref[...]
    wkp[1, shift:, :width] = wk_ref[...]
    wvt_val = wv_ref[...].T
    wvt[...] = jnp.zeros_like(wvt)
    wvt[0, :, :width] = wvt_val
    wvt[1, :, shift:] = wvt_val
    scale = math.log2(math.e) / math.sqrt(size)
    wq = wq_ref[...]
    gap = jnp.zeros((shift, width), BF16)
    q = jnp.concatenate(
        [
            jnp.dot(mine_ref[:half, :pad], jnp.concatenate([wq, gap], axis=0),
                    preferred_element_type=F32),
            jnp.dot(mine_ref[:half, 2 * width - pad:], jnp.concatenate([gap, wq], axis=0),
                    preferred_element_type=F32),
        ],
        axis=0,
    ) * scale
    qt = q.T.astype(BF16)
    qz[...] = jnp.zeros_like(qz)
    for h in range(HEADS):
        base = (h % 2) * size
        qz[h, base:base + size, :] = qt[h * size:(h + 1) * size]
    first = me * (rows // TILE)
    q_tile = first + lax.broadcasted_iota(jnp.int32, (tiles, rows), 1) // TILE
    k_tile = lax.broadcasted_iota(jnp.int32, (tiles, rows), 0)
    pick = (k_tile == q_tile).astype(BF16)
    seen = tn(visible_ref[...].astype(F32).astype(BF16), pick)
    own = (q_tile // TILES_VIEW) == (k_tile // TILES_VIEW)
    vis[...] = jnp.where((seen > 0.5) | own, F32(1.0), F32(0.0))
    m_s[...] = jnp.full_like(m_s, NEG)
    acc_s[...] = jnp.zeros_like(acc_s)


def absorb(x, wkp, wvt, qz, m_s, acc_s, width, vis_rows, limit):
    size = width // HEADS
    pad = lanes(width)
    half = x.shape[0]
    x_lo, x_hi = x[:, :pad], x[:, 2 * width - pad:]
    keys = jnp.concatenate(
        [
            jnp.dot(x_lo, wkp[0], preferred_element_type=F32).astype(BF16),
            jnp.dot(x_hi, wkp[1], preferred_element_type=F32).astype(BF16),
        ],
        axis=0,
    )
    values = [nt(wvt[0], x_lo).astype(BF16), nt(wvt[1], x_hi).astype(BF16)]
    ones = jnp.ones((16, half), BF16)
    for h in range(HEADS):
        s = jnp.dot(
            keys[:, (h // 2) * 128:(h // 2) * 128 + 128], qz[h], preferred_element_type=F32
        )
        m_old = m_s[h:h + 1, :]
        if vis_rows is None:
            part, at_lo, at_hi = limit
            ids = lax.broadcasted_iota(jnp.int32, (half, 1), 0)
            s = jnp.where(jnp.concatenate([at_lo(ids), at_hi(ids)], axis=0) < part, s, NEG)
            m_new = jnp.maximum(m_old, jnp.max(s, axis=0, keepdims=True))
            p = jnp.exp2(s - m_new).astype(BF16)
        else:
            tops = []
            for t, ok in enumerate(vis_rows):
                top = jnp.max(s[t * TILE:(t + 1) * TILE], axis=0, keepdims=True)
                tops.append(jnp.where(ok, top, NEG))
            m_new = functools.reduce(jnp.maximum, tops, m_old)
            parts = []
            for t, ok in enumerate(vis_rows):
                less = jnp.where(ok, m_new, F32(-NEG))
                parts.append(jnp.exp2(s[t * TILE:(t + 1) * TILE] - less).astype(BF16))
            p = jnp.concatenate(parts, axis=0)
        fade = jnp.exp2(m_old - m_new)
        m_s[h:h + 1, :] = m_new
        total = acc_s[h] * fade
        for k in range(2):
            v = jnp.concatenate([values[k][h * size:(h + 1) * size], ones], axis=0)
            total = total + jnp.dot(
                v, p[k * half:(k + 1) * half], preferred_element_type=F32
            )
        acc_s[h] = total


def finish(out_ref, wo_ref, acc_s, width):
    size = width // HEADS
    out = None
    for h in range(HEADS):
        mixed = (acc_s[h, :size] / acc_s[h, size:size + 1]).T.astype(BF16)
        term = jnp.dot(mixed, wo_ref[h * size:(h + 1) * size], preferred_element_type=F32)
        out = term if out is None else out + term
    out_ref[...] = out.astype(BF16)


def kernel(n, count_ref, mine_ref, visible_ref, wq_ref, wk_ref, wv_ref, wo_ref,
           out_ref, buf, wkp, wvt, qz, vis, m_s, acc_s, refs, send_sem, recv_sem, own_sem):
    width = mine_ref.shape[1] // 2
    rows = qz.shape[2]
    half = rows // 2
    ref_half = mine_ref.shape[0] - half
    tiles = rows // TILE
    me = lax.axis_index("seq")
    depth = n // 4
    core = lax.rem(me, 2)
    y = lax.rem(me // 2, 2)
    z = me // 4

    def index(zz, yy, cc):
        return (zz * 2 + yy) * 2 + cc

    peers = [index(z + 1, y, core), index(z - 1, y, core), index(z, 1 - y, core),
             index(z, y, 1 - core)]
    there = [z + 1 < depth, z >= 1, None, None]

    def copy(j, route, own=False):
        return pltpu.make_async_remote_copy(
            src_ref=mine_ref if own else buf.at[j],
            dst_ref=buf.at[j],
            send_sem=send_sem.at[route, j],
            recv_sem=recv_sem.at[j],
            device_id={"seq": peers[route]},
            device_id_type=pl.DeviceIdType.MESH,
        )

    barrier = pltpu.get_barrier_semaphore()

    def greet(peer):
        pl.semaphore_signal(barrier, inc=1, device_id={"seq": peer},
                            device_id_type=pl.DeviceIdType.MESH)

    for peer, ok in zip(peers, there):
        if ok is None:
            greet(peer)
        else:
            pl.when(ok)(functools.partial(greet, peer))
    pl.semaphore_wait(barrier, 2 + there[0].astype(jnp.int32) + there[1].astype(jnp.int32))

    for route in range(4):
        if there[route] is None:
            copy(me, route, True).start()
        else:
            pl.when(there[route])(lambda route=route: copy(me, route, True).start())
    keep = pltpu.make_async_copy(mine_ref, buf.at[me], own_sem)
    keep.start()
    prepare(mine_ref, visible_ref, wq_ref, wk_ref, wv_ref, wkp, wvt, qz, vis, m_s, acc_s, me)
    keep.wait()

    def nearest(k):
        low = jnp.minimum(z, depth - 1 - z)
        both = z + jnp.where(lax.rem(k, 2) == 1, (k + 1) // 2, -((k + 1) // 2))
        rest = jnp.where(z <= depth - 1 - z, k, depth - 1 - k)
        return jnp.where(k <= 2 * low, both, rest)

    def group(g, carry):
        for sign, route in ((-1, 0), (1, 1)):
            zz = z + sign * g

            @pl.when((g >= 1) & (zz >= 0) & (zz < depth))
            def _():
                j = index(zz, y, core)
                copy(j, 3).wait_recv()
                pl.when(there[route])(lambda: copy(j, route).start())
                copy(j, 2).start()
                copy(j, 3).start()

        for sign in (-1, 1):
            zz = z + sign * (g - 1)
            fits = (g >= 1) & (zz >= 0) & (zz < depth)

            @pl.when(fits if sign < 0 else fits & (g >= 2))
            def _():
                j = index(zz, 1 - y, core)
                copy(j, 3).wait_recv()
                copy(j, 3).start()

        def slot(s, carry):
            across = s // 2
            other = lax.rem(s, 2)
            k = g - across

            @pl.when((k >= 0) & (k < depth))
            def _():
                j = index(nearest(k), lax.rem(y + across, 2), lax.rem(core + other, 2))
                pl.when(other == 1)(lambda: copy(j, 3).wait_recv())
                vis_rows = [vis[pl.ds(j * tiles + t, 1), :] > 0.5 for t in range(tiles)]
                absorb(buf[j, :half], wkp, wvt, qz, m_s, acc_s, width, vis_rows, None)

            return carry

        return lax.fori_loop(0, 4, slot, carry)

    lax.fori_loop(0, depth + 1, group, 0)
    for j in range(n):
        refs[j * ref_half:(j + 1) * ref_half] = buf[j, half:]
    count = count_ref[0]
    block = half

    def ref_block(b, carry):
        def at(ids, extra):
            r = ids + b * block
            return (r // ref_half) * (2 * ref_half) + r % ref_half + extra
        absorb(refs[pl.ds(pl.multiple_of(b * block, block), block)], wkp, wvt, qz, m_s, acc_s,
               width, None, (count, lambda ids: at(ids, 0), lambda ids: at(ids, ref_half)))
        return carry

    lax.fori_loop(0, n * ref_half // block, ref_block, 0)
    finish(out_ref, wo_ref, acc_s, width)

    for route in range(4):
        if there[route] is None:
            copy(me, route, True).wait_send()
        else:
            pl.when(there[route])(lambda route=route: copy(me, route, True).wait_send())

    def drain(j, carry):
        zz, yy, cc = j // 4, lax.rem(j // 2, 2), lax.rem(j, 2)
        held = (cc == core) & (j != me)
        line = held & (yy == y)
        pl.when(line & (zz < z) & there[0])(lambda: copy(j, 0).wait_send())
        pl.when(line & (zz > z) & there[1])(lambda: copy(j, 1).wait_send())
        pl.when(line)(lambda: copy(j, 2).wait_send())
        pl.when(held)(lambda: copy(j, 3).wait_send())
        return carry

    lax.fori_loop(0, n, drain, 0)


def pack(x):
    half = x.shape[0] // 2
    return jnp.concatenate([x[:half], x[half:]], axis=1)


def local(hidden, ref_hidden, visible, ref_count, w_query, w_key, w_value, w_out):
    rows, width = hidden.shape
    size = width // HEADS
    pad = lanes(width)
    mine = jnp.concatenate([pack(hidden), pack(ref_hidden)], axis=0)
    n = lax.axis_size("seq")
    vmem = pl.BlockSpec(memory_space=pltpu.VMEM)
    return pl.pallas_call(
        functools.partial(kernel, n),
        out_shape=jax.ShapeDtypeStruct((rows, width), BF16),
        in_specs=[pl.BlockSpec(memory_space=pltpu.SMEM)] + [vmem] * 6,
        out_specs=vmem,
        scratch_shapes=[
            pltpu.VMEM((n,) + mine.shape, BF16),
            pltpu.VMEM((2, pad, pad), BF16),
            pltpu.VMEM((2, width, pad), BF16),
            pltpu.VMEM((HEADS, 128, rows), BF16),
            pltpu.VMEM((visible.shape[0], rows), F32),
            pltpu.VMEM((8, rows), F32),
            pltpu.VMEM((HEADS, size + 16, rows), F32),
            pltpu.VMEM((n * ref_hidden.shape[0] // 2, 2 * width), BF16),
            pltpu.SemaphoreType.DMA((4, n)),
            pltpu.SemaphoreType.DMA((n,)),
            pltpu.SemaphoreType.DMA,
        ],
        compiler_params=pltpu.CompilerParams(
            vmem_limit_bytes=56 << 20, collective_id=0, has_side_effects=True
        ),
    )(ref_count, mine, visible, w_query, w_key, w_value, w_out)


def solution(mesh):
    in_specs = (
        P(("groups", "seq"), None),
        P(("groups", "seq"), None),
        P("groups", None),
        P("groups"),
        P(),
        P(),
        P(),
        P(),
    )
    out_specs = P(("groups", "seq"), None)
    return jax.shard_map(local, mesh=mesh, in_specs=in_specs, out_specs=out_specs, check_vma=False)
```

```python
import functools
import math

import jax
import jax.numpy as jnp
from jax import lax
from jax.experimental import pallas as pl
from jax.experimental.pallas import tpu as pltpu
from jax.sharding import PartitionSpec as P

HEADS = 5
TILE = 128
TILES_VIEW = 8
NEG = -1e30
SPLIT = 1
AHEAD = 1
F32 = jnp.float32
BF16 = jnp.bfloat16


def lanes(width):
    return -(-width // 128) * 128


def nt(a, b):
    return lax.dot_general(a, b, (((1,), (1,)), ((), ())), preferred_element_type=F32)


def tn(a, b):
    return lax.dot_general(a, b, (((0,), (0,)), ((), ())), preferred_element_type=F32)


def prepare(mine_ref, visible_ref, wq_ref, wk_ref, wv_ref, wkp, wvt, qz, vis, m_s, acc_s, me):
    rows = qz.shape[2]
    half = rows // 2
    width = mine_ref.shape[1] // 2
    size = width // HEADS
    pad = lanes(width)
    shift = pad - width
    tiles = visible_ref.shape[0]
    wkp[...] = jnp.zeros_like(wkp)
    wkp[0, :width, :width] = wk_ref[...]
    wkp[1, shift:, :width] = wk_ref[...]
    wvt_val = wv_ref[...].T
    wvt[...] = jnp.zeros_like(wvt)
    wvt[0, :, :width] = wvt_val
    wvt[1, :, shift:] = wvt_val
    scale = math.log2(math.e) / math.sqrt(size)
    wq = wq_ref[...]
    gap = jnp.zeros((shift, width), BF16)
    q = jnp.concatenate(
        [
            jnp.dot(mine_ref[:half, :pad], jnp.concatenate([wq, gap], axis=0),
                    preferred_element_type=F32),
            jnp.dot(mine_ref[:half, 2 * width - pad:], jnp.concatenate([gap, wq], axis=0),
                    preferred_element_type=F32),
        ],
        axis=0,
    ) * scale
    qt = q.T.astype(BF16)
    qz[...] = jnp.zeros_like(qz)
    for h in range(HEADS):
        base = (h % 2) * size
        qz[h, base:base + size, :] = qt[h * size:(h + 1) * size]
    first = me * (rows // TILE)
    q_tile = first + lax.broadcasted_iota(jnp.int32, (tiles, rows), 1) // TILE
    k_tile = lax.broadcasted_iota(jnp.int32, (tiles, rows), 0)
    pick = (k_tile == q_tile).astype(BF16)
    seen = tn(visible_ref[...].astype(F32).astype(BF16), pick)
    own = (q_tile // TILES_VIEW) == (k_tile // TILES_VIEW)
    vis[...] = jnp.where((seen > 0.5) | own, F32(1.0), F32(0.0))
    m_s[...] = jnp.full_like(m_s, NEG)
    acc_s[...] = jnp.zeros_like(acc_s)


def absorb(x, wkp, wvt, qz, m_s, acc_s, width, vis_rows, limit):
    size = width // HEADS
    pad = lanes(width)
    half = x.shape[0]
    x_lo, x_hi = x[:, :pad], x[:, 2 * width - pad:]
    keys = jnp.concatenate(
        [
            jnp.dot(x_lo, wkp[0], preferred_element_type=F32).astype(BF16),
            jnp.dot(x_hi, wkp[1], preferred_element_type=F32).astype(BF16),
        ],
        axis=0,
    )
    values = [nt(wvt[0], x_lo).astype(BF16), nt(wvt[1], x_hi).astype(BF16)]
    ones = jnp.ones((16, half), BF16)
    rows = qz.shape[2]
    span = rows // SPLIT
    if limit is not None:
        part, at_lo, at_hi = limit
        ids = lax.broadcasted_iota(jnp.int32, (half, 1), 0)
        fits = jnp.concatenate([at_lo(ids), at_hi(ids)], axis=0) < part

    def score(h, cols):
        s = jnp.dot(
            keys[:, (h // 2) * 128:(h // 2) * 128 + 128], qz[h, :, cols],
            preferred_element_type=F32,
        )
        m_old = m_s[h:h + 1, cols]
        if vis_rows is None:
            s = jnp.where(fits, s, NEG)
            m_new = jnp.maximum(m_old, jnp.max(s, axis=0, keepdims=True))
            less = [m_new] * (2 * half // TILE)
        else:
            seen = [ok[:, cols] for ok in vis_rows]
            tops = [
                jnp.where(ok, jnp.max(s[t * TILE:(t + 1) * TILE], axis=0, keepdims=True), NEG)
                for t, ok in enumerate(seen)
            ]
            m_new = functools.reduce(jnp.maximum, tops, m_old)
            less = [jnp.where(ok, m_new, F32(-NEG)) for ok in seen]
        m_s[h:h + 1, cols] = m_new
        return s, less, jnp.exp2(m_old - m_new)

    def mix(h, cols, s, less, fade):
        p = jnp.concatenate(
            [
                jnp.exp2(s[t * TILE:(t + 1) * TILE] - row).astype(BF16)
                for t, row in enumerate(less)
            ],
            axis=0,
        )
        total = acc_s[h, :, cols] * fade
        for k in range(2):
            v = jnp.concatenate([values[k][h * size:(h + 1) * size], ones], axis=0)
            total = total + jnp.dot(
                v, p[k * half:(k + 1) * half], preferred_element_type=F32
            )
        acc_s[h, :, cols] = total

    units = [(h, slice(c * span, (c + 1) * span)) for h in range(HEADS) for c in range(SPLIT)]
    waiting = []
    for h, cols in units:
        waiting.append((h, cols) + score(h, cols))
        if len(waiting) > AHEAD:
            mix(*waiting.pop(0))
    for unit in waiting:
        mix(*unit)


def finish(out_ref, wo_ref, acc_s, width):
    size = width // HEADS
    out = None
    for h in range(HEADS):
        mixed = (acc_s[h, :size] / acc_s[h, size:size + 1]).T.astype(BF16)
        term = jnp.dot(mixed, wo_ref[h * size:(h + 1) * size], preferred_element_type=F32)
        out = term if out is None else out + term
    out_ref[...] = out.astype(BF16)


def kernel(n, count_ref, mine_ref, visible_ref, wq_ref, wk_ref, wv_ref, wo_ref,
           out_ref, buf, wkp, wvt, qz, vis, m_s, acc_s, refs, send_sem, recv_sem, own_sem):
    width = mine_ref.shape[1] // 2
    rows = qz.shape[2]
    half = rows // 2
    ref_half = mine_ref.shape[0] - half
    tiles = rows // TILE
    me = lax.axis_index("seq")
    depth = n // 4
    core = lax.rem(me, 2)
    y = lax.rem(me // 2, 2)
    z = me // 4

    def index(zz, yy, cc):
        return (zz * 2 + yy) * 2 + cc

    peers = [index(z + 1, y, core), index(z - 1, y, core), index(z, 1 - y, core),
             index(z, y, 1 - core)]
    there = [z + 1 < depth, z >= 1, None, None]

    def copy(j, route, own=False):
        return pltpu.make_async_remote_copy(
            src_ref=mine_ref if own else buf.at[j],
            dst_ref=buf.at[j],
            send_sem=send_sem.at[route, j],
            recv_sem=recv_sem.at[j],
            device_id={"seq": peers[route]},
            device_id_type=pl.DeviceIdType.MESH,
        )

    barrier = pltpu.get_barrier_semaphore()

    def greet(peer):
        pl.semaphore_signal(barrier, inc=1, device_id={"seq": peer},
                            device_id_type=pl.DeviceIdType.MESH)

    for peer, ok in zip(peers, there):
        if ok is None:
            greet(peer)
        else:
            pl.when(ok)(functools.partial(greet, peer))
    pl.semaphore_wait(barrier, 2 + there[0].astype(jnp.int32) + there[1].astype(jnp.int32))

    for route in range(4):
        if there[route] is None:
            copy(me, route, True).start()
        else:
            pl.when(there[route])(lambda route=route: copy(me, route, True).start())
    keep = pltpu.make_async_copy(mine_ref, buf.at[me], own_sem)
    keep.start()
    prepare(mine_ref, visible_ref, wq_ref, wk_ref, wv_ref, wkp, wvt, qz, vis, m_s, acc_s, me)
    keep.wait()

    def nearest(k):
        low = jnp.minimum(z, depth - 1 - z)
        both = z + jnp.where(lax.rem(k, 2) == 1, (k + 1) // 2, -((k + 1) // 2))
        rest = jnp.where(z <= depth - 1 - z, k, depth - 1 - k)
        return jnp.where(k <= 2 * low, both, rest)

    def group(g, carry):
        for sign, route in ((1, 1), (-1, 0)):
            zz = z + sign * g

            @pl.when((g >= 1) & (zz >= 0) & (zz < depth))
            def _():
                j = index(zz, y, core)
                copy(j, 3).wait_recv()
                pl.when(there[route])(lambda: copy(j, route).start())
                copy(j, 2).start()
                copy(j, 3).start()

        @pl.when(g >= 1)
        def _():
            j = index(nearest(g - 1), 1 - y, core)
            copy(j, 3).wait_recv()
            copy(j, 3).start()

        def slot(s, carry):
            across = s // 2
            other = lax.rem(s, 2)
            k = g - across

            @pl.when((k >= 0) & (k < depth))
            def _():
                j = index(nearest(k), lax.rem(y + across, 2), lax.rem(core + other, 2))
                pl.when(other == 1)(lambda: copy(j, 3).wait_recv())
                vis_rows = [vis[pl.ds(j * tiles + t, 1), :] > 0.5 for t in range(tiles)]
                absorb(buf[j, :half], wkp, wvt, qz, m_s, acc_s, width, vis_rows, None)

            return carry

        return lax.fori_loop(0, 4, slot, carry)

    lax.fori_loop(0, depth + 1, group, 0)
    for j in range(n):
        refs[j * ref_half:(j + 1) * ref_half] = buf[j, half:]
    count = count_ref[0]
    block = half

    def ref_block(b, carry):
        def at(ids, extra):
            r = ids + b * block
            return (r // ref_half) * (2 * ref_half) + r % ref_half + extra
        absorb(refs[pl.ds(pl.multiple_of(b * block, block), block)], wkp, wvt, qz, m_s, acc_s,
               width, None, (count, lambda ids: at(ids, 0), lambda ids: at(ids, ref_half)))
        return carry

    lax.fori_loop(0, n * ref_half // block, ref_block, 0)
    finish(out_ref, wo_ref, acc_s, width)

    for route in range(4):
        if there[route] is None:
            copy(me, route, True).wait_send()
        else:
            pl.when(there[route])(lambda route=route: copy(me, route, True).wait_send())

    def drain(j, carry):
        zz, yy, cc = j // 4, lax.rem(j // 2, 2), lax.rem(j, 2)
        held = (cc == core) & (j != me)
        line = held & (yy == y)
        pl.when(line & (zz < z) & there[0])(lambda: copy(j, 0).wait_send())
        pl.when(line & (zz > z) & there[1])(lambda: copy(j, 1).wait_send())
        pl.when(line)(lambda: copy(j, 2).wait_send())
        pl.when(held)(lambda: copy(j, 3).wait_send())
        return carry

    lax.fori_loop(0, n, drain, 0)


def pack(x):
    half = x.shape[0] // 2
    return jnp.concatenate([x[:half], x[half:]], axis=1)


def local(hidden, ref_hidden, visible, ref_count, w_query, w_key, w_value, w_out):
    rows, width = hidden.shape
    size = width // HEADS
    pad = lanes(width)
    mine = jnp.concatenate([pack(hidden), pack(ref_hidden)], axis=0)
    n = lax.axis_size("seq")
    vmem = pl.BlockSpec(memory_space=pltpu.VMEM)
    return pl.pallas_call(
        functools.partial(kernel, n),
        out_shape=jax.ShapeDtypeStruct((rows, width), BF16),
        in_specs=[pl.BlockSpec(memory_space=pltpu.SMEM)] + [vmem] * 6,
        out_specs=vmem,
        scratch_shapes=[
            pltpu.VMEM((n,) + mine.shape, BF16),
            pltpu.VMEM((2, pad, pad), BF16),
            pltpu.VMEM((2, width, pad), BF16),
            pltpu.VMEM((HEADS, 128, rows), BF16),
            pltpu.VMEM((visible.shape[0], rows), F32),
            pltpu.VMEM((8, rows), F32),
            pltpu.VMEM((HEADS, size + 16, rows), F32),
            pltpu.VMEM((n * ref_hidden.shape[0] // 2, 2 * width), BF16),
            pltpu.SemaphoreType.DMA((4, n)),
            pltpu.SemaphoreType.DMA((n,)),
            pltpu.SemaphoreType.DMA,
        ],
        compiler_params=pltpu.CompilerParams(
            vmem_limit_bytes=56 << 20, collective_id=0, has_side_effects=True
        ),
    )(ref_count, mine, visible, w_query, w_key, w_value, w_out)


def solution(mesh):
    in_specs = (
        P(("groups", "seq"), None),
        P(("groups", "seq"), None),
        P("groups", None),
        P("groups"),
        P(),
        P(),
        P(),
        P(),
    )
    out_specs = P(("groups", "seq"), None)
    return jax.shard_map(local, mesh=mesh, in_specs=in_specs, out_specs=out_specs, check_vma=False)
```

```python
import functools
import math

import jax
import jax.numpy as jnp
from jax import lax
from jax.experimental import pallas as pl
from jax.experimental.pallas import tpu as pltpu
from jax.sharding import PartitionSpec as P

HEADS = 5
TILE = 128
TILES_VIEW = 8
NEG = -1e30
SPLIT = 1
AHEAD = 1
F32 = jnp.float32
BF16 = jnp.bfloat16


def lanes(width):
    return -(-width // 128) * 128


def nt(a, b):
    return lax.dot_general(a, b, (((1,), (1,)), ((), ())), preferred_element_type=F32)


def tn(a, b):
    return lax.dot_general(a, b, (((0,), (0,)), ((), ())), preferred_element_type=F32)


def prepare(mine_ref, visible_ref, wq_ref, wk_ref, wv_ref, wkp, wvt, qz, vis, m_s, acc_s, me):
    rows = qz.shape[2]
    half = rows // 2
    width = mine_ref.shape[1] // 2
    size = width // HEADS
    pad = lanes(width)
    shift = pad - width
    tiles = visible_ref.shape[0]
    wkp[...] = jnp.zeros_like(wkp)
    wkp[0, :width, :width] = wk_ref[...]
    wkp[1, shift:, :width] = wk_ref[...]
    wvt_val = wv_ref[...].T
    wvt[...] = jnp.zeros_like(wvt)
    wvt[0, :, :width] = wvt_val
    wvt[1, :, shift:] = wvt_val
    scale = math.log2(math.e) / math.sqrt(size)
    wq = wq_ref[...]
    gap = jnp.zeros((shift, width), BF16)
    q = jnp.concatenate(
        [
            jnp.dot(mine_ref[:half, :pad], jnp.concatenate([wq, gap], axis=0),
                    preferred_element_type=F32),
            jnp.dot(mine_ref[:half, 2 * width - pad:], jnp.concatenate([gap, wq], axis=0),
                    preferred_element_type=F32),
        ],
        axis=0,
    ) * scale
    qt = q.T.astype(BF16)
    qz[...] = jnp.zeros_like(qz)
    for h in range(HEADS):
        base = (h % 2) * size
        qz[h, base:base + size, :] = qt[h * size:(h + 1) * size]
    first = me * (rows // TILE)
    q_tile = first + lax.broadcasted_iota(jnp.int32, (tiles, rows), 1) // TILE
    k_tile = lax.broadcasted_iota(jnp.int32, (tiles, rows), 0)
    pick = (k_tile == q_tile).astype(BF16)
    seen = tn(visible_ref[...].astype(F32).astype(BF16), pick)
    own = (q_tile // TILES_VIEW) == (k_tile // TILES_VIEW)
    vis[...] = jnp.where((seen > 0.5) | own, F32(1.0), F32(0.0))
    m_s[...] = jnp.full_like(m_s, NEG)
    acc_s[...] = jnp.zeros_like(acc_s)


def absorb(x, wkp, wvt, qz, m_s, acc_s, width, vis_rows, limit):
    size = width // HEADS
    pad = lanes(width)
    half = x.shape[0]
    x_lo, x_hi = x[:, :pad], x[:, 2 * width - pad:]
    keys = jnp.concatenate(
        [
            jnp.dot(x_lo, wkp[0], preferred_element_type=F32).astype(BF16),
            jnp.dot(x_hi, wkp[1], preferred_element_type=F32).astype(BF16),
        ],
        axis=0,
    )
    values = []
    ones = jnp.ones((16, half), BF16)
    rows = qz.shape[2]
    span = rows // SPLIT
    if limit is not None:
        part, at_lo, at_hi = limit
        ids = lax.broadcasted_iota(jnp.int32, (half, 1), 0)
        fits = jnp.concatenate([at_lo(ids), at_hi(ids)], axis=0) < part

    def score(h, cols):
        s = jnp.dot(
            keys[:, (h // 2) * 128:(h // 2) * 128 + 128], qz[h, :, cols],
            preferred_element_type=F32,
        )
        m_old = m_s[h:h + 1, cols]
        if vis_rows is None:
            s = jnp.where(fits, s, NEG)
            m_new = jnp.maximum(m_old, jnp.max(s, axis=0, keepdims=True))
            less = [m_new] * (2 * half // TILE)
        else:
            seen = [ok[:, cols] for ok in vis_rows]
            tops = [
                jnp.where(ok, jnp.max(s[t * TILE:(t + 1) * TILE], axis=0, keepdims=True), NEG)
                for t, ok in enumerate(seen)
            ]
            m_new = functools.reduce(jnp.maximum, tops, m_old)
            less = [jnp.where(ok, m_new, F32(-NEG)) for ok in seen]
        m_s[h:h + 1, cols] = m_new
        return s, less, jnp.exp2(m_old - m_new)

    def mix(h, cols, s, less, fade):
        if not values:
            values.append(nt(wvt[0], x_lo).astype(BF16))
            values.append(nt(wvt[1], x_hi).astype(BF16))
        p = jnp.concatenate(
            [
                jnp.exp2(s[t * TILE:(t + 1) * TILE] - row).astype(BF16)
                for t, row in enumerate(less)
            ],
            axis=0,
        )
        total = acc_s[h, :, cols] * fade
        for k in range(2):
            v = jnp.concatenate([values[k][h * size:(h + 1) * size], ones], axis=0)
            total = total + jnp.dot(
                v, p[k * half:(k + 1) * half], preferred_element_type=F32
            )
        acc_s[h, :, cols] = total

    units = [(h, slice(c * span, (c + 1) * span)) for h in range(HEADS) for c in range(SPLIT)]
    waiting = []
    for h, cols in units:
        waiting.append((h, cols) + score(h, cols))
        if len(waiting) > AHEAD:
            mix(*waiting.pop(0))
    for unit in waiting:
        mix(*unit)


def finish(out_ref, wo_ref, acc_s, width):
    size = width // HEADS
    out = None
    for h in range(HEADS):
        mixed = (acc_s[h, :size] / acc_s[h, size:size + 1]).T.astype(BF16)
        term = jnp.dot(mixed, wo_ref[h * size:(h + 1) * size], preferred_element_type=F32)
        out = term if out is None else out + term
    out_ref[...] = out.astype(BF16)


def kernel(n, count_ref, mine_ref, visible_ref, wq_ref, wk_ref, wv_ref, wo_ref,
           out_ref, buf, wkp, wvt, qz, vis, m_s, acc_s, refs, send_sem, recv_sem, own_sem):
    width = mine_ref.shape[1] // 2
    rows = qz.shape[2]
    half = rows // 2
    ref_half = mine_ref.shape[0] - half
    tiles = rows // TILE
    me = lax.axis_index("seq")
    depth = n // 4
    core = lax.rem(me, 2)
    y = lax.rem(me // 2, 2)
    z = me // 4

    def index(zz, yy, cc):
        return (zz * 2 + yy) * 2 + cc

    peers = [index(z + 1, y, core), index(z - 1, y, core), index(z, 1 - y, core),
             index(z, y, 1 - core)]
    there = [z + 1 < depth, z >= 1, None, None]

    def copy(j, route, own=False):
        return pltpu.make_async_remote_copy(
            src_ref=mine_ref if own else buf.at[j],
            dst_ref=buf.at[j],
            send_sem=send_sem.at[route, j],
            recv_sem=recv_sem.at[j],
            device_id={"seq": peers[route]},
            device_id_type=pl.DeviceIdType.MESH,
        )

    barrier = pltpu.get_barrier_semaphore()

    def greet(peer):
        pl.semaphore_signal(barrier, inc=1, device_id={"seq": peer},
                            device_id_type=pl.DeviceIdType.MESH)

    for peer, ok in zip(peers, there):
        if ok is None:
            greet(peer)
        else:
            pl.when(ok)(functools.partial(greet, peer))
    pl.semaphore_wait(barrier, 2 + there[0].astype(jnp.int32) + there[1].astype(jnp.int32))

    for route in range(4):
        if there[route] is None:
            copy(me, route, True).start()
        else:
            pl.when(there[route])(lambda route=route: copy(me, route, True).start())
    keep = pltpu.make_async_copy(mine_ref, buf.at[me], own_sem)
    keep.start()
    prepare(mine_ref, visible_ref, wq_ref, wk_ref, wv_ref, wkp, wvt, qz, vis, m_s, acc_s, me)
    keep.wait()

    def nearest(k):
        low = jnp.minimum(z, depth - 1 - z)
        both = z + jnp.where(lax.rem(k, 2) == 1, (k + 1) // 2, -((k + 1) // 2))
        rest = jnp.where(z <= depth - 1 - z, k, depth - 1 - k)
        return jnp.where(k <= 2 * low, both, rest)

    def group(g, carry):
        for sign, route in ((1, 1), (-1, 0)):
            zz = z + sign * g

            @pl.when((g >= 1) & (zz >= 0) & (zz < depth))
            def _():
                j = index(zz, y, core)
                copy(j, 3).wait_recv()
                pl.when(there[route])(lambda: copy(j, route).start())
                copy(j, 2).start()
                copy(j, 3).start()

        def slot(s, carry):
            across = s // 2
            other = lax.rem(s, 2)
            k = g - across

            @pl.when((k >= 0) & (k < depth))
            def _():
                j = index(nearest(k), lax.rem(y + across, 2), lax.rem(core + other, 2))
                pl.when((other == 1) | (across == 1))(lambda: copy(j, 3).wait_recv())
                pl.when((other == 0) & (across == 1))(lambda: copy(j, 3).start())
                vis_rows = [vis[pl.ds(j * tiles + t, 1), :] > 0.5 for t in range(tiles)]
                absorb(buf[j, :half], wkp, wvt, qz, m_s, acc_s, width, vis_rows, None)

            return carry

        return lax.fori_loop(0, 4, slot, carry)

    lax.fori_loop(0, depth + 1, group, 0)
    for j in range(n):
        refs[j * ref_half:(j + 1) * ref_half] = buf[j, half:]
    count = count_ref[0]
    block = half

    def ref_block(b, carry):
        def at(ids, extra):
            r = ids + b * block
            return (r // ref_half) * (2 * ref_half) + r % ref_half + extra
        absorb(refs[pl.ds(pl.multiple_of(b * block, block), block)], wkp, wvt, qz, m_s, acc_s,
               width, None, (count, lambda ids: at(ids, 0), lambda ids: at(ids, ref_half)))
        return carry

    lax.fori_loop(0, n * ref_half // block, ref_block, 0)
    finish(out_ref, wo_ref, acc_s, width)

    for route in range(4):
        if there[route] is None:
            copy(me, route, True).wait_send()
        else:
            pl.when(there[route])(lambda route=route: copy(me, route, True).wait_send())

    def drain(j, carry):
        zz, yy, cc = j // 4, lax.rem(j // 2, 2), lax.rem(j, 2)
        held = (cc == core) & (j != me)
        line = held & (yy == y)
        pl.when(line & (zz < z) & there[0])(lambda: copy(j, 0).wait_send())
        pl.when(line & (zz > z) & there[1])(lambda: copy(j, 1).wait_send())
        pl.when(line)(lambda: copy(j, 2).wait_send())
        pl.when(held)(lambda: copy(j, 3).wait_send())
        return carry

    lax.fori_loop(0, n, drain, 0)


def pack(x):
    half = x.shape[0] // 2
    return jnp.concatenate([x[:half], x[half:]], axis=1)


def local(hidden, ref_hidden, visible, ref_count, w_query, w_key, w_value, w_out):
    rows, width = hidden.shape
    size = width // HEADS
    pad = lanes(width)
    mine = jnp.concatenate([pack(hidden), pack(ref_hidden)], axis=0)
    n = lax.axis_size("seq")
    vmem = pl.BlockSpec(memory_space=pltpu.VMEM)
    return pl.pallas_call(
        functools.partial(kernel, n),
        out_shape=jax.ShapeDtypeStruct((rows, width), BF16),
        in_specs=[pl.BlockSpec(memory_space=pltpu.SMEM)] + [vmem] * 6,
        out_specs=vmem,
        scratch_shapes=[
            pltpu.VMEM((n,) + mine.shape, BF16),
            pltpu.VMEM((2, pad, pad), BF16),
            pltpu.VMEM((2, width, pad), BF16),
            pltpu.VMEM((HEADS, 128, rows), BF16),
            pltpu.VMEM((visible.shape[0], rows), F32),
            pltpu.VMEM((8, rows), F32),
            pltpu.VMEM((HEADS, size + 16, rows), F32),
            pltpu.VMEM((n * ref_hidden.shape[0] // 2, 2 * width), BF16),
            pltpu.SemaphoreType.DMA((4, n)),
            pltpu.SemaphoreType.DMA((n,)),
            pltpu.SemaphoreType.DMA,
        ],
        compiler_params=pltpu.CompilerParams(
            vmem_limit_bytes=56 << 20, collective_id=0, has_side_effects=True
        ),
    )(ref_count, mine, visible, w_query, w_key, w_value, w_out)


def solution(mesh):
    in_specs = (
        P(("groups", "seq"), None),
        P(("groups", "seq"), None),
        P("groups", None),
        P("groups"),
        P(),
        P(),
        P(),
        P(),
    )
    out_specs = P(("groups", "seq"), None)
    return jax.shard_map(local, mesh=mesh, in_specs=in_specs, out_specs=out_specs, check_vma=False)
```

```python
import functools
import math

import jax
import jax.numpy as jnp
from jax import lax
from jax.experimental import pallas as pl
from jax.experimental.pallas import tpu as pltpu
from jax.sharding import PartitionSpec as P

HEADS = 5
TILE = 128
TILES_VIEW = 8
NEG = -1e30
SPLIT = 1
AHEAD = 1
F32 = jnp.float32
BF16 = jnp.bfloat16


def lanes(width):
    return -(-width // 128) * 128


def nt(a, b):
    return lax.dot_general(a, b, (((1,), (1,)), ((), ())), preferred_element_type=F32)


def tn(a, b):
    return lax.dot_general(a, b, (((0,), (0,)), ((), ())), preferred_element_type=F32)


def prepare(mine_ref, visible_ref, wq_ref, wk_ref, wv_ref, wkp, wvt, qz, vis, m_s, acc_s, me):
    rows = qz.shape[2]
    half = rows // 2
    width = mine_ref.shape[1] // 2
    size = width // HEADS
    pad = lanes(width)
    shift = pad - width
    tiles = visible_ref.shape[0]
    wkp[...] = jnp.zeros_like(wkp)
    wkp[0, :width, :width] = wk_ref[...]
    wkp[1, shift:, :width] = wk_ref[...]
    wvt_val = wv_ref[...].T
    wvt[...] = jnp.zeros_like(wvt)
    wvt[0, :, :width] = wvt_val
    wvt[1, :, shift:] = wvt_val
    scale = math.log2(math.e) / math.sqrt(size)
    wq = wq_ref[...]
    gap = jnp.zeros((shift, width), BF16)
    q = jnp.concatenate(
        [
            jnp.dot(mine_ref[:half, :pad], jnp.concatenate([wq, gap], axis=0),
                    preferred_element_type=F32),
            jnp.dot(mine_ref[:half, 2 * width - pad:], jnp.concatenate([gap, wq], axis=0),
                    preferred_element_type=F32),
        ],
        axis=0,
    ) * scale
    qt = q.T.astype(BF16)
    qz[...] = jnp.zeros_like(qz)
    for h in range(HEADS):
        base = (h % 2) * size
        qz[h, base:base + size, :] = qt[h * size:(h + 1) * size]
    first = me * (rows // TILE)
    q_tile = first + lax.broadcasted_iota(jnp.int32, (tiles, rows), 1) // TILE
    k_tile = lax.broadcasted_iota(jnp.int32, (tiles, rows), 0)
    pick = (k_tile == q_tile).astype(BF16)
    seen = tn(visible_ref[...].astype(F32).astype(BF16), pick)
    own = (q_tile // TILES_VIEW) == (k_tile // TILES_VIEW)
    vis[...] = jnp.where((seen > 0.5) | own, F32(1.0), F32(0.0))
    m_s[...] = jnp.full_like(m_s, NEG)
    acc_s[...] = jnp.zeros_like(acc_s)


def absorb(x, wkp, wvt, qz, m_s, acc_s, width, vis_rows, limit):
    size = width // HEADS
    pad = lanes(width)
    half = x.shape[0]
    x_lo, x_hi = x[:, :pad], x[:, 2 * width - pad:]
    keys = jnp.concatenate(
        [
            jnp.dot(x_lo, wkp[0], preferred_element_type=F32).astype(BF16),
            jnp.dot(x_hi, wkp[1], preferred_element_type=F32).astype(BF16),
        ],
        axis=0,
    )
    values = []
    ones = jnp.ones((16, half), BF16)
    rows = qz.shape[2]
    span = rows // SPLIT
    if limit is not None:
        part, at_lo, at_hi = limit
        ids = lax.broadcasted_iota(jnp.int32, (half, 1), 0)
        fits = jnp.concatenate([at_lo(ids), at_hi(ids)], axis=0) < part

    def score(h, cols):
        s = jnp.dot(
            keys[:, (h // 2) * 128:(h // 2) * 128 + 128], qz[h, :, cols],
            preferred_element_type=F32,
        )
        m_old = m_s[h:h + 1, cols]
        if vis_rows is None:
            s = jnp.where(fits, s, NEG)
            m_new = jnp.maximum(m_old, jnp.max(s, axis=0, keepdims=True))
            less = [m_new] * (2 * half // TILE)
        else:
            seen = [ok[:, cols] for ok in vis_rows]
            tops = [
                jnp.where(ok, jnp.max(s[t * TILE:(t + 1) * TILE], axis=0, keepdims=True), NEG)
                for t, ok in enumerate(seen)
            ]
            m_new = functools.reduce(jnp.maximum, tops, m_old)
            less = [jnp.where(ok, m_new, F32(-NEG)) for ok in seen]
        m_s[h:h + 1, cols] = m_new
        return s, less, jnp.exp2(m_old - m_new)

    def mix(h, cols, s, less, fade):
        if not values:
            values.append(nt(wvt[0], x_lo).astype(BF16))
            values.append(nt(wvt[1], x_hi).astype(BF16))
        p = jnp.concatenate(
            [
                jnp.exp2(s[t * TILE:(t + 1) * TILE] - row).astype(BF16)
                for t, row in enumerate(less)
            ],
            axis=0,
        )
        total = acc_s[h, :, cols] * fade
        for k in range(2):
            v = jnp.concatenate([values[k][h * size:(h + 1) * size], ones], axis=0)
            total = total + jnp.dot(
                v, p[k * half:(k + 1) * half], preferred_element_type=F32
            )
        acc_s[h, :, cols] = total

    units = [(h, slice(c * span, (c + 1) * span)) for h in range(HEADS) for c in range(SPLIT)]
    waiting = []
    for h, cols in units:
        waiting.append((h, cols) + score(h, cols))
        if len(waiting) > AHEAD:
            mix(*waiting.pop(0))
    for unit in waiting:
        mix(*unit)


def finish(out_ref, wo_ref, acc_s, width):
    size = width // HEADS
    out = None
    for h in range(HEADS):
        mixed = (acc_s[h, :size] / acc_s[h, size:size + 1]).astype(BF16)
        term = tn(wo_ref[h * size:(h + 1) * size], mixed)
        out = term if out is None else out + term
    out_ref[...] = out.astype(BF16)


def kernel(n, count_ref, mine_ref, visible_ref, wq_ref, wk_ref, wv_ref, wo_ref,
           out_ref, buf, wkp, wvt, qz, vis, m_s, acc_s, refs, send_sem, recv_sem, own_sem):
    width = mine_ref.shape[1] // 2
    rows = qz.shape[2]
    half = rows // 2
    ref_half = mine_ref.shape[0] - half
    tiles = rows // TILE
    me = lax.axis_index("seq")
    depth = n // 4
    core = lax.rem(me, 2)
    y = lax.rem(me // 2, 2)
    z = me // 4

    def index(zz, yy, cc):
        return (zz * 2 + yy) * 2 + cc

    peers = [index(z + 1, y, core), index(z - 1, y, core), index(z, 1 - y, core),
             index(z, y, 1 - core)]
    there = [z + 1 < depth, z >= 1, None, None]

    def copy(j, route, own=False):
        return pltpu.make_async_remote_copy(
            src_ref=mine_ref if own else buf.at[j],
            dst_ref=buf.at[j],
            send_sem=send_sem.at[route, j],
            recv_sem=recv_sem.at[j],
            device_id={"seq": peers[route]},
            device_id_type=pl.DeviceIdType.MESH,
        )

    barrier = pltpu.get_barrier_semaphore()

    def greet(peer):
        pl.semaphore_signal(barrier, inc=1, device_id={"seq": peer},
                            device_id_type=pl.DeviceIdType.MESH)

    for peer, ok in zip(peers, there):
        if ok is None:
            greet(peer)
        else:
            pl.when(ok)(functools.partial(greet, peer))
    pl.semaphore_wait(barrier, 2 + there[0].astype(jnp.int32) + there[1].astype(jnp.int32))

    for route in range(4):
        if there[route] is None:
            copy(me, route, True).start()
        else:
            pl.when(there[route])(lambda route=route: copy(me, route, True).start())
    keep = pltpu.make_async_copy(mine_ref, buf.at[me], own_sem)
    keep.start()
    prepare(mine_ref, visible_ref, wq_ref, wk_ref, wv_ref, wkp, wvt, qz, vis, m_s, acc_s, me)
    keep.wait()

    def nearest(k):
        low = jnp.minimum(z, depth - 1 - z)
        both = z + jnp.where(lax.rem(k, 2) == 1, (k + 1) // 2, -((k + 1) // 2))
        rest = jnp.where(z <= depth - 1 - z, k, depth - 1 - k)
        return jnp.where(k <= 2 * low, both, rest)

    def group(g, carry):
        for sign, route in ((1, 1), (-1, 0)):
            zz = z + sign * g

            @pl.when((g >= 1) & (zz >= 0) & (zz < depth))
            def _():
                j = index(zz, y, core)
                copy(j, 3).wait_recv()
                pl.when(there[route])(lambda: copy(j, route).start())
                copy(j, 2).start()
                copy(j, 3).start()

        def slot(s, carry):
            across = s // 2
            other = lax.rem(s, 2)
            k = g - across

            @pl.when((k >= 0) & (k < depth))
            def _():
                j = index(nearest(k), lax.rem(y + across, 2), lax.rem(core + other, 2))
                pl.when((other == 1) | (across == 1))(lambda: copy(j, 3).wait_recv())
                pl.when((other == 0) & (across == 1))(lambda: copy(j, 3).start())
                vis_rows = [vis[pl.ds(j * tiles + t, 1), :] > 0.5 for t in range(tiles)]
                absorb(buf[j, :half], wkp, wvt, qz, m_s, acc_s, width, vis_rows, None)

            return carry

        return lax.fori_loop(0, 4, slot, carry)

    lax.fori_loop(0, depth + 1, group, 0)
    for j in range(n):
        refs[j * ref_half:(j + 1) * ref_half] = buf[j, half:]
    count = count_ref[0]
    block = half

    def ref_block(b, carry):
        def at(ids, extra):
            r = ids + b * block
            return (r // ref_half) * (2 * ref_half) + r % ref_half + extra
        absorb(refs[pl.ds(pl.multiple_of(b * block, block), block)], wkp, wvt, qz, m_s, acc_s,
               width, None, (count, lambda ids: at(ids, 0), lambda ids: at(ids, ref_half)))
        return carry

    lax.fori_loop(0, n * ref_half // block, ref_block, 0)
    finish(out_ref, wo_ref, acc_s, width)

    for route in range(4):
        if there[route] is None:
            copy(me, route, True).wait_send()
        else:
            pl.when(there[route])(lambda route=route: copy(me, route, True).wait_send())

    def drain(j, carry):
        zz, yy, cc = j // 4, lax.rem(j // 2, 2), lax.rem(j, 2)
        held = (cc == core) & (j != me)
        line = held & (yy == y)
        pl.when(line & (zz < z) & there[0])(lambda: copy(j, 0).wait_send())
        pl.when(line & (zz > z) & there[1])(lambda: copy(j, 1).wait_send())
        pl.when(line)(lambda: copy(j, 2).wait_send())
        pl.when(held)(lambda: copy(j, 3).wait_send())
        return carry

    lax.fori_loop(0, n, drain, 0)


def pack(x):
    half = x.shape[0] // 2
    return jnp.concatenate([x[:half], x[half:]], axis=1)


def local(hidden, ref_hidden, visible, ref_count, w_query, w_key, w_value, w_out):
    rows, width = hidden.shape
    size = width // HEADS
    pad = lanes(width)
    mine = jnp.concatenate([pack(hidden), pack(ref_hidden)], axis=0)
    n = lax.axis_size("seq")
    vmem = pl.BlockSpec(memory_space=pltpu.VMEM)
    return pl.pallas_call(
        functools.partial(kernel, n),
        out_shape=jax.ShapeDtypeStruct((width, rows), BF16),
        in_specs=[pl.BlockSpec(memory_space=pltpu.SMEM)] + [vmem] * 6,
        out_specs=vmem,
        scratch_shapes=[
            pltpu.VMEM((n,) + mine.shape, BF16),
            pltpu.VMEM((2, pad, pad), BF16),
            pltpu.VMEM((2, width, pad), BF16),
            pltpu.VMEM((HEADS, 128, rows), BF16),
            pltpu.VMEM((visible.shape[0], rows), F32),
            pltpu.VMEM((8, rows), F32),
            pltpu.VMEM((HEADS, size + 16, rows), F32),
            pltpu.VMEM((n * ref_hidden.shape[0] // 2, 2 * width), BF16),
            pltpu.SemaphoreType.DMA((4, n)),
            pltpu.SemaphoreType.DMA((n,)),
            pltpu.SemaphoreType.DMA,
        ],
        compiler_params=pltpu.CompilerParams(
            vmem_limit_bytes=56 << 20, collective_id=0, has_side_effects=True
        ),
    )(ref_count, mine, visible, w_query, w_key, w_value, w_out).T


def solution(mesh):
    in_specs = (
        P(("groups", "seq"), None),
        P(("groups", "seq"), None),
        P("groups", None),
        P("groups"),
        P(),
        P(),
        P(),
        P(),
    )
    out_specs = P(("groups", "seq"), None)
    return jax.shard_map(local, mesh=mesh, in_specs=in_specs, out_specs=out_specs, check_vma=False)
```
